32 devices in a mesh: span: 8 (over y, x, core), chord: 4 (over z).
Axes of the slice: x: 2, y: 2, z: 4, core: 2. Of those that a mesh axis runs over, the one named last changes fastest.
Arguments:
- start_block: float32 [64, 24576], P(None, ('span', 'chord')), may hold values from -6 to 6
- blocks: bfloat16 [4608, 128, 128], P(('span', 'chord')), may hold values from -0.032958984 to 0.032958984
- blk_col: int32 [4608], P(('span', 'chord')), may hold values from 0 to 25, as said below
- block_scale: float32 [4608], P(('span', 'chord')), may hold values from 0.5 to 2
Outputs:
- filtered: float32 [64, 24576], P(None, ('span', 'chord'))
The draws below stay inside these ranges and needn't reach their ends.
Inputs may be any that keep to these rules, and one draw needn't show every extreme that they name: `blk_col`: each slot codes o * 6 + r with o in 0 to 4. With o = 0, r is at least the slot's own block row within its tile; with o > 0, r is below 2. Tiles at the last span position use only o = 0 or 1.
All inputs are finite; a program needn't handle non-finite values.
Results may differ from the reference program's by a relative error of at most 0.014.
Values may be sent and summed in bfloat16 or wider, within the bound.
A program may use at most 64 MiB of HBM per device.

```python
import math
import jax
import jax.numpy as jnp
from jax import lax

BS = 128
COLS = 64
BPR = 24
RB = 6
HB = 2
DEG = 3
TILES_SPAN = 8
TILES_CHORD = 4
NBLK = 144
SLOTS = 4608
NODES = 24576


def draw_blk_col(key, part):
    slots = jnp.arange(SLOTS, dtype=jnp.int32)
    tile = slots // NBLK
    at_tip = tile // TILES_CHORD == TILES_SPAN - 1
    block_row = slots % NBLK // BPR
    offset_key, place_key = jax.random.split(key)
    offset_draw = jax.random.randint(offset_key, (SLOTS,), 0, 5)
    offset = jnp.where(at_tip, offset_draw % 2, offset_draw)
    place_draw = jax.random.randint(place_key, (SLOTS,), 0, 1 << 20)
    within = jnp.where(offset == 0, block_row + place_draw % (RB - block_row), place_draw % HB)
    return (offset * RB + within).astype(jnp.int32)


def level_of(own_key, extent, cuts, least, largest):
    loudness = 1.0
    for position, parts in cuts:
        heights = jax.random.uniform(jax.random.fold_in(jax.random.fold_in(own_key, 6), position), (parts,), jnp.float32, least / len(cuts), largest / len(cuts))
        loudness = loudness * jnp.repeat(jnp.exp(heights), extent[position] // parts).reshape((-1,) + (1,) * (len(extent) - 1 - position))
    return loudness


def normal_values(own_key, dims, spread, reach, cuts=(), held_as=jnp.bfloat16):
    loudness = level_of(own_key, dims, cuts, -0.22, 0.18) if cuts else 1.0
    entries = jax.random.normal(own_key, dims, jnp.float32) * spread * loudness
    return jnp.minimum(jnp.maximum(entries, -reach), reach).astype(held_as)


def setup_inputs(seed: int = 0) -> dict:
    keys = jax.random.split(jax.random.key(seed), 5)
    start_block = normal_values(keys[0], (COLS, NODES), 1.0, 6.0, ((1, 32),), jnp.float32)
    blocks = normal_values(keys[1], (SLOTS, BS, BS), (0.43 / (2 * BPR * BS) ** 0.5), 0.032958984, ((0, 32),))
    blk_col = draw_blk_col(jax.random.fold_in(keys[4], 71), 0)
    block_scale = jnp.clip(jnp.exp(math.log(2.0) - 1.3862944 * jax.random.uniform(keys[3], (SLOTS,), jnp.float32) ** level_of(keys[3], (SLOTS,), ((0, 32),), -0.2, 0.2)), 0.5, 2.0)
    return dict(start_block=start_block, blocks=blocks, blk_col=blk_col, block_scale=block_scale)


SPAN_STEP = (0, 0, 1, 1, 1)
CHORD_STEP = (0, 1, -1, 0, 1)
SPREAD = 0.8

def block_indices(blk_col):
    slots = jnp.arange(SLOTS, dtype=jnp.int32)
    tile = slots // NBLK
    span_pos = tile // TILES_CHORD
    chord_pos = tile % TILES_CHORD
    offset = blk_col // RB
    within = blk_col % RB
    span_step = jnp.array(SPAN_STEP, dtype=jnp.int32)[offset]
    chord_step = jnp.array(CHORD_STEP, dtype=jnp.int32)[offset]
    target = (span_pos + span_step) * TILES_CHORD + (chord_pos + chord_step) % TILES_CHORD
    columns = (target * RB + within).astype(jnp.int32)
    row_index = (tile * RB + slots % NBLK // BPR).astype(jnp.int32)
    return (row_index.reshape(-1, NBLK), columns.reshape(-1, NBLK))

def apply_operator(vectors, blocks, block_scale, row_index, columns):
    narrowed = vectors.astype(jnp.bfloat16).reshape(COLS, -1, BS)

    def visit(summed, pieces):
        tile_blocks, tile_scale, tile_rows, tile_cols = pieces
        widened = tile_blocks.astype(jnp.float32)
        across = narrowed[:, tile_cols, :].astype(jnp.float32)
        row_vals = narrowed[:, tile_rows, :].astype(jnp.float32)
        forward = jnp.einsum('cnk,nrk->cnr', across, widened) * tile_scale[None, :, None]
        mirror = jnp.einsum('cnr,nrk->cnk', row_vals, widened) * tile_scale[None, :, None]
        summed = summed.at[:, tile_rows, :].add(forward).at[:, tile_cols, :].add(mirror)
        return (summed, None)
    summed = jnp.zeros((COLS, NODES // BS, BS), jnp.float32)
    summed = lax.scan(visit, summed, (blocks.reshape(-1, NBLK, BS, BS), block_scale.reshape(-1, NBLK), row_index, columns))[0]
    return summed.reshape(COLS, NODES)

def chebyshev(vectors, operate):
    earlier = vectors
    current = operate(vectors) / SPREAD
    for degree in range(DEG - 1):
        following = 2.0 * operate(current) / SPREAD - earlier
        earlier, current = (current, following)
    return current

def reference(start_block, blocks, blk_col, block_scale):
    row_index, columns = block_indices(blk_col)

    def operate(vectors):
        return apply_operator(vectors, blocks, block_scale, row_index, columns)
    filtered_once = chebyshev(start_block, operate)
    gram = jnp.dot(filtered_once, filtered_once.T, precision=lax.Precision.HIGHEST) / NODES
    factor = jnp.linalg.cholesky(gram)
    inverse = lax.linalg.triangular_solve(factor, jnp.eye(COLS, dtype=jnp.float32), left_side=True, lower=True)
    normed_basis = jnp.dot(inverse, filtered_once, precision=lax.Precision.HIGHEST)
    return chebyshev(normed_basis, operate)
```

```python
import functools

import jax
import jax.numpy as jnp
from jax import lax
from jax.experimental import pallas as pl
from jax.experimental.pallas import tpu as pltpu
from jax.sharding import PartitionSpec as P

BS = 128
COLS = 64
BPR = 24
RB = 6
HB = 2
DEG = 3
SPREAD = 0.8
RIMS = 4
EDGE = HB * BS
OWN = RB * BS
WIDE = OWN + RIMS * EDGE
PLACES = RB + RIMS * HB
NONE = BPR
APPS = 2 * DEG
GROUPS = 2
PART = COLS // GROUPS
PAIR = 3
PANEL = 4
HIGH = lax.Precision.HIGHEST
MESH = pl.DeviceIdType.MESH
FIRST = ((1, 0), (1, 3), (0, 1), (1, 1), (1, 2), (0, 3), (0, 0), (0, 2))
LAST = ((1, 1), (0, 3), (0, 0), (1, 3), (1, 0), (1, 2), (0, 1), (0, 2))
MIDDLE = ((1, 3), (1, 1), (1, 0), (1, 2), (0, 3), (0, 1), (0, 0), (0, 2))
NN = (((1,), (0,)), ((), ()))
NT = (((1,), (1,)), ((), ()))


def mm(a, b, dims=NN):
    return lax.dot_general(a, b, dims, preferred_element_type=jnp.float32)


def pointers(column_ref, point_ref):
    subs = lax.broadcasted_iota(jnp.int32, (8, BS), 0)
    lanes = lax.broadcasted_iota(jnp.int32, (8, BS), 1)
    own = [subs == i for i in range(RB)]
    places = []
    for n in range(BPR):
        column = jnp.zeros((8, BS), jnp.int32)
        for i in range(RB):
            column = jnp.where(own[i], column_ref[i * BPR + n], column)
        p = column
        for o in range(2, RIMS + 1):
            p = p - jnp.where(column >= o * RB, RB - HB, 0)
        places.append(p)
    mine = jnp.full((8, BS), -1, jnp.int32)
    for n in range(BPR):
        mine = jnp.where(lanes == n, places[n], mine)
    earlier = jnp.full((8, BS), NONE, jnp.int32)
    final = jnp.full((8, BS), NONE, jnp.int32)
    for n in range(BPR):
        earlier = jnp.where((mine == places[n]) & (lanes > n), n, earlier)
        final = jnp.where(lanes == places[n], n, final)
    point_ref[0] = earlier
    point_ref[1] = final


def densify(step, point_ref, scale_ref, blocks_ref, dense_ref, sums):
    half = BS // 2
    for n in range(BPR):
        for row in range(PAIR):
            i = step * PAIR + row
            earlier = point_ref[0, i, n]
            scale = scale_ref[i * BPR + n]
            for h in range(2):
                block = blocks_ref[i * BPR + n, h * half : (h + 1) * half, :]
                partial = sums[2 * row + h]
                partial[n] = partial[earlier] + block.astype(jnp.float32) * scale
    for row in range(PAIR):
        i = step * PAIR + row
        for p in range(PLACES):
            final = point_ref[1, i, p]
            for h in range(2):
                top = i * BS + h * half
                dense_ref[top : top + half, p * BS : (p + 1) * BS] = sums[2 * row + h][final].astype(jnp.bfloat16)


def inverse_factor(gram):
    rows = lax.broadcasted_iota(jnp.int32, (COLS, COLS), 0)
    cols = lax.broadcasted_iota(jnp.int32, (COLS, COLS), 1)
    eye = (rows == cols).astype(jnp.float32)
    work = jnp.concatenate([gram, eye], axis=1)
    index = lax.broadcasted_iota(jnp.int32, (COLS, 2 * COLS), 0)
    done = []
    for start in range(0, COLS, PANEL):
        base = start // 8 * 8
        if start % 8 == 0 and start:
            done.append(work[:8])
            work = work[8:]
        panel = [jnp.broadcast_to(work[:, k : k + 1], work.shape) for k in range(start, start + PANEL)]
        for j in range(PANEL):
            at = start + j - base
            scale = 1.0 / panel[j][at : at + 1]
            factor = jnp.where(index[base:] > start + j, panel[j], 0.0)
            for later in range(j + 1, PANEL):
                panel[later] = panel[later] - factor * (panel[later][at : at + 1] * scale)
            work = work - factor * (work[at : at + 1] * scale)
    done.append(work)
    work = jnp.concatenate(done, axis=0)
    diagonal = jnp.sum(jnp.where(rows == cols, work[:, :COLS], 0.0), axis=1, keepdims=True)
    return work[:, COLS:] / jnp.sqrt(diagonal)


def filters(
    spans, chords,
    start_hbm, blocks_hbm, column_hbm, scale_hbm, out_ref,
    start_ref, start_sem, blocks_ref, blocks_sem, column_ref, column_sem, scale_ref, scale_sem,
    lanes_ref, point_ref, point_sem, sums_a, sums_b, sums_c, sums_d, sums_e, sums_f,
    dense_ref, across, mutual, prev, cur, total, edge, given, rims, back, inverse,
    chord_parts, span_parts,
    edge_send, edge_recv, back_send, back_recv,
    chord_send, chord_recv, span_send, span_recv,
):
    s = lax.axis_index("span")
    c = lax.axis_index("chord")
    after = lax.rem(c + 1, chords)
    before = lax.rem(c + chords - 1, chords)
    last = spans - 1

    columns = pltpu.make_async_copy(column_hbm, column_ref, column_sem)
    columns.start()
    scales = pltpu.make_async_copy(scale_hbm, scale_ref, scale_sem)
    scales.start()
    chunk = PAIR * BPR
    fetches = [
        pltpu.make_async_copy(
            blocks_hbm.at[q * chunk : (q + 1) * chunk], blocks_ref.at[q * chunk : (q + 1) * chunk], blocks_sem.at[q]
        )
        for q in range(RB // PAIR)
    ]
    for fetch in fetches:
        fetch.start()
    begin = pltpu.make_async_copy(start_hbm, start_ref, start_sem)
    begin.start()

    barrier = pltpu.get_barrier_semaphore()

    def greet(a, b):
        pl.semaphore_signal(barrier, inc=1, device_id=(a, b), device_id_type=MESH)

    for step in range(1, chords):
        greet(s, lax.rem(c + step, chords))
    for step in range(1, spans):
        greet(lax.rem(s + step, spans), c)

    @pl.when(s > 0)
    def _():
        greet(s - 1, before)
        greet(s - 1, after)

    @pl.when(s < last)
    def _():
        greet(s + 1, before)
        greet(s + 1, after)

    columns.wait()
    pointers(column_ref, lanes_ref)
    move = pltpu.make_async_copy(lanes_ref, point_ref, point_sem)
    move.start()
    sums = (sums_a, sums_b, sums_c, sums_d, sums_e, sums_f)
    for partial in sums:
        partial[NONE] = jnp.zeros(partial.shape[1:], jnp.float32)

    @pl.when(s == last)
    def _():
        rims[:, :, 1:] = jnp.zeros(rims[:, :, 1:].shape, rims.dtype)

    @pl.when(s == 0)
    def _():
        back[:, :, 1:] = jnp.zeros(back[:, :, 1:].shape, back.dtype)

    prev[...] = jnp.zeros_like(prev)
    scales.wait()
    move.wait()
    for q in range(RB // PAIR):
        fetches[q].wait()
        densify(q, point_ref, scale_ref, blocks_ref, dense_ref, sums)
    begin.wait()
    for g in range(GROUPS):
        cur[g] = start_ref[g * PART : (g + 1) * PART, :]
    corners = 2 * (jnp.minimum(s, 1) + jnp.minimum(last - s, 1))
    down = jnp.maximum(s - 1, 0)
    up = jnp.minimum(s + 1, last)
    edge_to = [(s, before), (down, after), (down, c), (down, before)]
    back_to = [(s, after), (up, before), (up, c), (up, after)]

    def edge_copy(k, g, o):
        return pltpu.make_async_remote_copy(
            src_ref=edge.at[k, g], dst_ref=rims.at[k, g, o],
            send_sem=edge_send.at[k, g, o], recv_sem=edge_recv.at[k, g, o],
            device_id=edge_to[o], device_id_type=MESH,
        )

    def back_copy(k, g, o):
        return pltpu.make_async_remote_copy(
            src_ref=given.at[k, g, o], dst_ref=back.at[k, g, o],
            send_sem=back_send.at[k, g, o], recv_sem=back_recv.at[k, g, o],
            device_id=back_to[o], device_id_type=MESH,
        )

    def chord_copy(step):
        return pltpu.make_async_remote_copy(
            src_ref=chord_parts.at[c], dst_ref=chord_parts.at[c],
            send_sem=chord_send.at[step], recv_sem=chord_recv.at[step],
            device_id=(s, lax.rem(c + step, chords)), device_id_type=MESH,
        )

    def span_copy(step):
        return pltpu.make_async_remote_copy(
            src_ref=span_parts.at[s], dst_ref=span_parts.at[s],
            send_sem=span_send.at[step], recv_sem=span_recv.at[step],
            device_id=(lax.rem(s + step, spans), c), device_id_type=MESH,
        )

    def halo(o, inner, outer):
        if o == 0:
            inner()
        else:
            pl.when(outer)(inner)

    def rim_dense(o):
        return dense_ref[:, OWN + o * EDGE : OWN + (o + 1) * EDGE]

    def give(k, g, o, narrowed):
        given[k, g, o] = mm(narrowed, rim_dense(o)).astype(jnp.bfloat16)

    def send(k, g, ready=False):
        if not ready:
            edge[k, g] = cur[g, :, :EDGE].astype(jnp.bfloat16)
        narrowed = cur[g].astype(jnp.bfloat16)

        def issue(steps):
            for out, o in steps:
                if out:
                    halo(o, lambda o=o: edge_copy(k, g, o).start(), s > 0)
                else:
                    if not ready:
                        give(k, g, o, narrowed)
                    halo(o, lambda o=o: back_copy(k, g, o).start(), s < last)

        pl.when(c == 0)(lambda: issue(FIRST))
        pl.when(c == chords - 1)(lambda: issue(LAST))
        pl.when((c > 0) & (c < chords - 1))(lambda: issue(MIDDLE))
        if isinstance(k, int):
            for q in range(RB // HB):
                lo, hi = q * EDGE, (q + 1) * EDGE
                total[g, :, lo:hi] = mm(narrowed[:, :hi], dense_ref[:hi, lo:hi]) + mm(
                    narrowed[:, lo:], dense_ref[lo:hi, lo:OWN], NT
                )
        else:
            total[g] = mm(narrowed, mutual[...])

    def receive(k, g):
        for o in (2, 0, 1, 3):
            halo(o, lambda o=o: edge_copy(k, g, o).wait_recv(), s < last)
        seen = jnp.concatenate([rims[k, g, o] for o in range(RIMS)], axis=1)
        applied = total[g] + mm(seen, across[...])
        for o in (2, 0, 1, 3):
            halo(o, lambda o=o: back_copy(k, g, o).wait_recv(), s > 0)
        returned = back[k, g, 0].astype(jnp.float32)
        for o in range(1, RIMS):
            returned = returned + back[k, g, o].astype(jnp.float32)
        applied = jnp.concatenate([applied[:, :EDGE] + returned, applied[:, EDGE:]], axis=1)
        first = lax.rem(k, DEG) == 0
        gain = jnp.where(first, 1.0 / SPREAD, 2.0 / SPREAD)
        keep = jnp.where(first, 0.0, 1.0)
        following = applied * gain - prev[g] * keep
        prev[g] = cur[g]
        cur[g] = following

    narrowed = cur[0].astype(jnp.bfloat16)
    edge[0, 0] = narrowed[:, :EDGE]
    for o in range(RIMS):
        give(0, 0, o, narrowed)
    pl.semaphore_wait(barrier, chords - 1 + spans - 1 + corners)
    for g in range(GROUPS):
        send(0, g, ready=g == 0)

    rows = lax.broadcasted_iota(jnp.int32, (EDGE, EDGE), 0)
    cols = lax.broadcasted_iota(jnp.int32, (EDGE, EDGE), 1)
    eye = (rows == cols).astype(jnp.bfloat16)
    for o in range(RIMS):
        across[o * EDGE : (o + 1) * EDGE, :] = mm(eye, rim_dense(o), NT).astype(jnp.bfloat16)
    for q in range(RB // HB):
        lo, hi = q * EDGE, (q + 1) * EDGE
        turned = mm(eye, dense_ref[:, lo:hi], NT)
        mutual[lo:hi, :] = (dense_ref[lo:hi, :OWN].astype(jnp.float32) + turned).astype(jnp.bfloat16)

    def drain(k):
        for g in range(GROUPS):
            for o in range(RIMS):
                halo(o, lambda o=o: edge_copy(k, g, o).wait_send(), s > 0)
                halo(o, lambda o=o: back_copy(k, g, o).wait_send(), s < last)

    def advance(k, carry):
        for g in range(GROUPS):
            receive(k - 1, g)
            send(k, g)

        @pl.when(k == DEG)
        def _():
            basis = cur[...].reshape(COLS, OWN)
            gram = lax.dot_general(basis, basis, NT, precision=HIGH, preferred_element_type=jnp.float32)
            chord_parts[c] = jnp.concatenate([gram[: COLS // 2], gram[COLS // 2 :]], axis=1)
            for step in range(1, chords):
                chord_copy(step).start()

        @pl.when(k == DEG + 1)
        def _():
            for step in range(1, chords):
                chord_copy(step).wait_recv()
            part = chord_parts[0]
            for step in range(1, chords):
                part = part + chord_parts[step]
            span_parts[s] = part
            for step in range(1, spans):
                span_copy(step).start()

        @pl.when(k == DEG + 2)
        def _():
            for step in range(1, spans):
                span_copy(step).wait_recv()
            part = span_parts[0]
            for step in range(1, spans):
                part = part + span_parts[step]
            part = part / float(OWN * spans * chords)
            gram = jnp.concatenate([part[:, :COLS], part[:, COLS:]], axis=0)
            inverse[...] = inverse_factor(gram)

        drain(k - 1)
        return carry

    lax.fori_loop(1, APPS, advance, 0)
    for g in range(GROUPS):
        receive(jnp.int32(APPS - 1), g)
    basis = cur[...].reshape(COLS, OWN)
    out_ref[...] = jnp.dot(inverse[...], basis, precision=HIGH, preferred_element_type=jnp.float32)
    drain(APPS - 1)
    for step in range(1, chords):
        chord_copy(step).wait_send()
    for step in range(1, spans):
        span_copy(step).wait_send()


def on_device(spans, chords, start_block, blocks, blk_col, block_scale):
    vmem = pl.BlockSpec(memory_space=pltpu.VMEM)
    dma = pltpu.SemaphoreType.DMA
    halves = (COLS // 2, 2 * COLS)
    split = (GROUPS, PART, OWN)
    flags = (APPS, GROUPS, RIMS)
    halos = flags + (PART, EDGE)
    return pl.pallas_call(
        functools.partial(filters, spans, chords),
        out_shape=jax.ShapeDtypeStruct((COLS, OWN), jnp.float32),
        in_specs=[pl.BlockSpec(memory_space=pl.ANY)] * 4,
        out_specs=vmem,
        scratch_shapes=[
            pltpu.VMEM((COLS, OWN), jnp.float32),
            dma,
            pltpu.VMEM(blocks.shape, jnp.bfloat16),
            dma((RB // PAIR,)),
            pltpu.SMEM(blk_col.shape, jnp.int32),
            dma,
            pltpu.SMEM(block_scale.shape, jnp.float32),
            dma,
            pltpu.VMEM((2, 8, BS), jnp.int32),
            pltpu.SMEM((2, 8, BS), jnp.int32),
            dma,
            *[pltpu.VMEM((BPR + 1, BS // 2, BS), jnp.float32)] * (2 * PAIR),
            pltpu.VMEM((OWN, WIDE), jnp.bfloat16),
            pltpu.VMEM((RIMS * EDGE, OWN), jnp.bfloat16),
            pltpu.VMEM((OWN, OWN), jnp.bfloat16),
            pltpu.VMEM(split, jnp.float32),
            pltpu.VMEM(split, jnp.float32),
            pltpu.VMEM(split, jnp.float32),
            pltpu.VMEM((APPS, GROUPS, PART, EDGE), jnp.bfloat16),
            pltpu.VMEM(halos, jnp.bfloat16),
            pltpu.VMEM(halos, jnp.bfloat16),
            pltpu.VMEM(halos, jnp.bfloat16),
            pltpu.VMEM((COLS, COLS), jnp.float32),
            pltpu.VMEM((chords,) + halves, jnp.float32),
            pltpu.VMEM((spans,) + halves, jnp.float32),
            dma(flags), dma(flags), dma(flags), dma(flags),
            dma((chords,)), dma((chords,)), dma((spans,)), dma((spans,)),
        ],
        compiler_params=pltpu.CompilerParams(
            collective_id=0, has_side_effects=True, vmem_limit_bytes=62 * 1024 * 1024
        ),
        name="filters",
    )(start_block, blocks, blk_col, block_scale)


def solution(mesh):
    in_specs = (
        P(None, ("span", "chord")),
        P(("span", "chord"), None, None),
        P(("span", "chord")),
        P(("span", "chord")),
    )
    out_specs = P(None, ("span", "chord"))
    return jax.shard_map(
        functools.partial(on_device, mesh.shape["span"], mesh.shape["chord"]),
        mesh=mesh, in_specs=in_specs, out_specs=out_specs, check_vma=False,
    )
```

```python
import functools

import jax
import jax.numpy as jnp
from jax import lax
from jax.experimental import pallas as pl
from jax.experimental.pallas import tpu as pltpu
from jax.sharding import PartitionSpec as P

BS = 128
COLS = 64
BPR = 24
RB = 6
HB = 2
DEG = 3
SPREAD = 0.8
RIMS = 4
EDGE = HB * BS
OWN = RB * BS
WIDE = OWN + RIMS * EDGE
PLACES = RB + RIMS * HB
NONE = BPR
APPS = 2 * DEG
GROUPS = 2
PART = COLS // GROUPS
PAIR = 3
STRIP = COLS // 4
PANEL = 4
HIGH = lax.Precision.HIGHEST
MESH = pl.DeviceIdType.MESH
FIRST = ((1, 0), (1, 3), (0, 1), (1, 1), (1, 2), (0, 3), (0, 0), (0, 2))
LAST = ((1, 1), (0, 3), (0, 0), (1, 3), (1, 0), (1, 2), (0, 1), (0, 2))
MIDDLE = ((1, 3), (1, 1), (1, 0), (1, 2), (0, 3), (0, 1), (0, 0), (0, 2))
NN = (((1,), (0,)), ((), ()))
NT = (((1,), (1,)), ((), ()))


def mm(a, b, dims=NN):
    return lax.dot_general(a, b, dims, preferred_element_type=jnp.float32)


def pointers(column_ref, point_ref):
    subs = lax.broadcasted_iota(jnp.int32, (8, BS), 0)
    lanes = lax.broadcasted_iota(jnp.int32, (8, BS), 1)
    own = [subs == i for i in range(RB)]
    places = []
    for n in range(BPR):
        column = jnp.zeros((8, BS), jnp.int32)
        for i in range(RB):
            column = jnp.where(own[i], column_ref[i * BPR + n], column)
        p = column
        for o in range(2, RIMS + 1):
            p = p - jnp.where(column >= o * RB, RB - HB, 0)
        places.append(p)
    mine = jnp.full((8, BS), -1, jnp.int32)
    for n in range(BPR):
        mine = jnp.where(lanes == n, places[n], mine)
    earlier = jnp.full((8, BS), NONE, jnp.int32)
    final = jnp.full((8, BS), NONE, jnp.int32)
    for n in range(BPR):
        earlier = jnp.where((mine == places[n]) & (lanes > n), n, earlier)
        final = jnp.where(lanes == places[n], n, final)
    point_ref[0] = earlier
    point_ref[1] = final


def densify(step, point_ref, scale_ref, blocks_ref, dense_ref, sums):
    half = BS // 2
    for n in range(BPR):
        for row in range(PAIR):
            i = step * PAIR + row
            earlier = point_ref[0, i, n]
            scale = scale_ref[i * BPR + n]
            for h in range(2):
                block = blocks_ref[i * BPR + n, h * half : (h + 1) * half, :]
                partial = sums[2 * row + h]
                partial[n] = partial[earlier] + block.astype(jnp.float32) * scale
    for row in range(PAIR):
        i = step * PAIR + row
        for p in range(PLACES):
            final = point_ref[1, i, p]
            for h in range(2):
                top = i * BS + h * half
                dense_ref[top : top + half, p * BS : (p + 1) * BS] = sums[2 * row + h][final].astype(jnp.bfloat16)


def inverse_factor(gram):
    rows = lax.broadcasted_iota(jnp.int32, (COLS, COLS), 0)
    cols = lax.broadcasted_iota(jnp.int32, (COLS, COLS), 1)
    eye = (rows == cols).astype(jnp.float32)
    work = jnp.concatenate([gram, eye], axis=1)
    index = lax.broadcasted_iota(jnp.int32, (COLS, 2 * COLS), 0)
    done = []
    for start in range(0, COLS, PANEL):
        base = start // 8 * 8
        if start % 8 == 0 and start:
            done.append(work[:8])
            work = work[8:]
        panel = [jnp.broadcast_to(work[:, k : k + 1], work.shape) for k in range(start, start + PANEL)]
        for j in range(PANEL):
            at = start + j - base
            scale = 1.0 / panel[j][at : at + 1]
            factor = jnp.where(index[base:] > start + j, panel[j], 0.0)
            for later in range(j + 1, PANEL):
                panel[later] = panel[later] - factor * (panel[later][at : at + 1] * scale)
            work = work - factor * (work[at : at + 1] * scale)
    done.append(work)
    work = jnp.concatenate(done, axis=0)
    diagonal = jnp.sum(jnp.where(rows == cols, work[:, :COLS], 0.0), axis=1, keepdims=True)
    return work[:, COLS:] / jnp.sqrt(diagonal)


def pack(gram):
    rows = [gram[i * STRIP : (i + 1) * STRIP, i * STRIP :] for i in range(4)]
    quarter = STRIP // 4
    return jnp.concatenate(
        [
            jnp.concatenate([rows[0], rows[1], rows[3]], axis=1),
            jnp.concatenate([rows[2][j * quarter : (j + 1) * quarter] for j in range(4)], axis=1),
        ],
        axis=0,
    )


def unpack(packed):
    top, tail = packed[:STRIP], packed[STRIP:]
    wide = 2 * STRIP
    rows = [
        top[:, :COLS],
        top[:, COLS : 2 * COLS - STRIP],
        jnp.concatenate([tail[:, j * wide : (j + 1) * wide] for j in range(4)], axis=0),
        top[:, 2 * COLS - STRIP :],
    ]
    upper = jnp.concatenate(
        [rows[0]]
        + [jnp.concatenate([jnp.zeros((STRIP, i * STRIP), jnp.float32), rows[i]], axis=1) for i in range(1, 4)],
        axis=0,
    )
    down = lax.broadcasted_iota(jnp.int32, (COLS, COLS), 0) // STRIP
    right = lax.broadcasted_iota(jnp.int32, (COLS, COLS), 1) // STRIP
    return jnp.where(right >= down, upper, upper.T)


def filters(
    spans, chords,
    start_hbm, blocks_hbm, column_hbm, scale_hbm, out_ref,
    start_ref, start_sem, blocks_ref, blocks_sem, column_ref, column_sem, scale_ref, scale_sem,
    lanes_ref, point_ref, point_sem, sums_a, sums_b, sums_c, sums_d, sums_e, sums_f,
    dense_ref, across, mutual, prev, cur, total, edge, given, rims, back, inverse,
    chord_parts, span_parts,
    edge_send, edge_recv, back_send, back_recv,
    chord_send, chord_recv, span_send, span_recv,
):
    s = lax.axis_index("span")
    c = lax.axis_index("chord")
    after = lax.rem(c + 1, chords)
    before = lax.rem(c + chords - 1, chords)
    last = spans - 1

    barrier = pltpu.get_barrier_semaphore()

    def greet(a, b):
        pl.semaphore_signal(barrier, inc=1, device_id=(a, b), device_id_type=MESH)

    @pl.when(s > 0)
    def _():
        greet(s - 1, before)
        greet(s - 1, after)

    @pl.when(s < last)
    def _():
        greet(s + 1, before)
        greet(s + 1, after)

    for step in (1, chords - 1, *range(2, chords - 1)):
        greet(s, lax.rem(c + step, chords))
    for step in (1, spans - 1, *range(2, spans - 1)):
        greet(lax.rem(s + step, spans), c)

    columns = pltpu.make_async_copy(column_hbm, column_ref, column_sem)
    columns.start()
    scales = pltpu.make_async_copy(scale_hbm, scale_ref, scale_sem)
    scales.start()
    chunk = PAIR * BPR
    fetches = [
        pltpu.make_async_copy(
            blocks_hbm.at[q * chunk : (q + 1) * chunk], blocks_ref.at[q * chunk : (q + 1) * chunk], blocks_sem.at[q]
        )
        for q in range(RB // PAIR)
    ]
    for fetch in fetches:
        fetch.start()
    begin = pltpu.make_async_copy(start_hbm, start_ref, start_sem)
    begin.start()

    columns.wait()
    pointers(column_ref, lanes_ref)
    move = pltpu.make_async_copy(lanes_ref, point_ref, point_sem)
    move.start()
    sums = (sums_a, sums_b, sums_c, sums_d, sums_e, sums_f)
    for partial in sums:
        partial[NONE] = jnp.zeros(partial.shape[1:], jnp.float32)

    @pl.when(s == last)
    def _():
        rims[:, :, 1:] = jnp.zeros(rims[:, :, 1:].shape, rims.dtype)

    @pl.when(s == 0)
    def _():
        back[:, :, 1:] = jnp.zeros(back[:, :, 1:].shape, back.dtype)

    prev[...] = jnp.zeros_like(prev)
    scales.wait()
    move.wait()
    for q in range(RB // PAIR):
        fetches[q].wait()
        densify(q, point_ref, scale_ref, blocks_ref, dense_ref, sums)
    begin.wait()
    for g in range(GROUPS):
        cur[g] = start_ref[g * PART : (g + 1) * PART, :]
    corners = 2 * (jnp.minimum(s, 1) + jnp.minimum(last - s, 1))
    down = jnp.maximum(s - 1, 0)
    up = jnp.minimum(s + 1, last)
    edge_to = [(s, before), (down, after), (down, c), (down, before)]
    back_to = [(s, after), (up, before), (up, c), (up, after)]

    def edge_copy(k, g, o):
        return pltpu.make_async_remote_copy(
            src_ref=edge.at[k, g], dst_ref=rims.at[k, g, o],
            send_sem=edge_send.at[k, g, o], recv_sem=edge_recv.at[k, g, o],
            device_id=edge_to[o], device_id_type=MESH,
        )

    def back_copy(k, g, o):
        return pltpu.make_async_remote_copy(
            src_ref=given.at[k, g, o], dst_ref=back.at[k, g, o],
            send_sem=back_send.at[k, g, o], recv_sem=back_recv.at[k, g, o],
            device_id=back_to[o], device_id_type=MESH,
        )

    def chord_copy(step):
        return pltpu.make_async_remote_copy(
            src_ref=chord_parts.at[c], dst_ref=chord_parts.at[c],
            send_sem=chord_send.at[step], recv_sem=chord_recv.at[step],
            device_id=(s, lax.rem(c + step, chords)), device_id_type=MESH,
        )

    def span_copy(step):
        return pltpu.make_async_remote_copy(
            src_ref=span_parts.at[s], dst_ref=span_parts.at[s],
            send_sem=span_send.at[step], recv_sem=span_recv.at[step],
            device_id=(lax.rem(s + step, spans), c), device_id_type=MESH,
        )

    def halo(o, inner, outer):
        if o == 0:
            inner()
        else:
            pl.when(outer)(inner)

    def rim_dense(o):
        return dense_ref[:, OWN + o * EDGE : OWN + (o + 1) * EDGE]

    def give(k, g, o, narrowed):
        given[k, g, o] = mm(narrowed, rim_dense(o)).astype(jnp.bfloat16)

    def send(k, g, ready=False):
        if not ready:
            edge[k, g] = cur[g, :, :EDGE].astype(jnp.bfloat16)
        narrowed = cur[g].astype(jnp.bfloat16)

        def issue(steps):
            for out, o in steps:
                if out:
                    halo(o, lambda o=o: edge_copy(k, g, o).start(), s > 0)
                else:
                    if not ready:
                        give(k, g, o, narrowed)
                    halo(o, lambda o=o: back_copy(k, g, o).start(), s < last)

        pl.when(c == 0)(lambda: issue(FIRST))
        pl.when(c == chords - 1)(lambda: issue(LAST))
        pl.when((c > 0) & (c < chords - 1))(lambda: issue(MIDDLE))
        if isinstance(k, int):
            for q in range(RB // HB):
                lo, hi = q * EDGE, (q + 1) * EDGE
                total[g, :, lo:hi] = mm(narrowed[:, :hi], dense_ref[:hi, lo:hi]) + mm(
                    narrowed[:, lo:], dense_ref[lo:hi, lo:OWN], NT
                )
        else:
            total[g] = mm(narrowed, mutual[...])

    def receive(k, g):
        for o in (2, 0, 1, 3):
            halo(o, lambda o=o: edge_copy(k, g, o).wait_recv(), s < last)
        seen = jnp.concatenate([rims[k, g, o] for o in range(RIMS)], axis=1)
        applied = total[g] + mm(seen, across[...])
        for o in (2, 0, 1, 3):
            halo(o, lambda o=o: back_copy(k, g, o).wait_recv(), s > 0)
        returned = back[k, g, 0].astype(jnp.float32)
        for o in range(1, RIMS):
            returned = returned + back[k, g, o].astype(jnp.float32)
        applied = jnp.concatenate([applied[:, :EDGE] + returned, applied[:, EDGE:]], axis=1)
        first = lax.rem(k, DEG) == 0
        gain = jnp.where(first, 1.0 / SPREAD, 2.0 / SPREAD)
        keep = jnp.where(first, 0.0, 1.0)
        following = applied * gain - prev[g] * keep
        prev[g] = cur[g]
        cur[g] = following

    narrowed = cur[0].astype(jnp.bfloat16)
    edge[0, 0] = narrowed[:, :EDGE]
    for o in range(RIMS):
        give(0, 0, o, narrowed)
    pl.semaphore_wait(barrier, chords - 1 + spans - 1 + corners)
    for g in range(GROUPS):
        send(0, g, ready=g == 0)

    rows = lax.broadcasted_iota(jnp.int32, (EDGE, EDGE), 0)
    cols = lax.broadcasted_iota(jnp.int32, (EDGE, EDGE), 1)
    eye = (rows == cols).astype(jnp.bfloat16)
    for o in range(RIMS):
        across[o * EDGE : (o + 1) * EDGE, :] = mm(eye, rim_dense(o), NT).astype(jnp.bfloat16)
    for q in range(RB // HB):
        lo, hi = q * EDGE, (q + 1) * EDGE
        turned = mm(eye, dense_ref[:, lo:hi], NT)
        mutual[lo:hi, :] = (dense_ref[lo:hi, :OWN].astype(jnp.float32) + turned).astype(jnp.bfloat16)

    def drain(k):
        for g in range(GROUPS):
            for o in range(RIMS):
                halo(o, lambda o=o: edge_copy(k, g, o).wait_send(), s > 0)
                halo(o, lambda o=o: back_copy(k, g, o).wait_send(), s < last)

    def advance(k, carry):
        for g in range(GROUPS):
            receive(k - 1, g)
            send(k, g)

        @pl.when(k == DEG)
        def _():
            basis = cur[...].reshape(COLS, OWN)
            gram = lax.dot_general(basis, basis, NT, precision=HIGH, preferred_element_type=jnp.float32)
            chord_parts[c] = pack(gram)
            for step in range(1, chords):
                chord_copy(step).start()

        @pl.when(k == DEG + 1)
        def _():
            for step in range(1, chords):
                chord_copy(step).wait_recv()
            part = chord_parts[0]
            for step in range(1, chords):
                part = part + chord_parts[step]
            span_parts[s] = part
            for step in range(1, spans):
                span_copy(step).start()

        @pl.when(k == DEG + 2)
        def _():
            for step in range(1, spans):
                span_copy(step).wait_recv()
            part = span_parts[0]
            for step in range(1, spans):
                part = part + span_parts[step]
            part = part / float(OWN * spans * chords)
            inverse[...] = inverse_factor(unpack(part))

        drain(k - 1)
        return carry

    lax.fori_loop(1, APPS, advance, 0)
    for g in range(GROUPS):
        receive(jnp.int32(APPS - 1), g)
    basis = cur[...].reshape(COLS, OWN)
    out_ref[...] = jnp.dot(inverse[...], basis, precision=HIGH, preferred_element_type=jnp.float32)
    drain(APPS - 1)
    for step in range(1, chords):
        chord_copy(step).wait_send()
    for step in range(1, spans):
        span_copy(step).wait_send()


def on_device(spans, chords, start_block, blocks, blk_col, block_scale):
    vmem = pl.BlockSpec(memory_space=pltpu.VMEM)
    dma = pltpu.SemaphoreType.DMA
    packed = (STRIP + STRIP // 4, 2 * COLS)
    split = (GROUPS, PART, OWN)
    flags = (APPS, GROUPS, RIMS)
    halos = flags + (PART, EDGE)
    return pl.pallas_call(
        functools.partial(filters, spans, chords),
        out_shape=jax.ShapeDtypeStruct((COLS, OWN), jnp.float32),
        in_specs=[pl.BlockSpec(memory_space=pl.ANY)] * 4,
        out_specs=vmem,
        scratch_shapes=[
            pltpu.VMEM((COLS, OWN), jnp.float32),
            dma,
            pltpu.VMEM(blocks.shape, jnp.bfloat16),
            dma((RB // PAIR,)),
            pltpu.SMEM(blk_col.shape, jnp.int32),
            dma,
            pltpu.SMEM(block_scale.shape, jnp.float32),
            dma,
            pltpu.VMEM((2, 8, BS), jnp.int32),
            pltpu.SMEM((2, 8, BS), jnp.int32),
            dma,
            *[pltpu.VMEM((BPR + 1, BS // 2, BS), jnp.float32)] * (2 * PAIR),
            pltpu.VMEM((OWN, WIDE), jnp.bfloat16),
            pltpu.VMEM((RIMS * EDGE, OWN), jnp.bfloat16),
            pltpu.VMEM((OWN, OWN), jnp.bfloat16),
            pltpu.VMEM(split, jnp.float32),
            pltpu.VMEM(split, jnp.float32),
            pltpu.VMEM(split, jnp.float32),
            pltpu.VMEM((APPS, GROUPS, PART, EDGE), jnp.bfloat16),
            pltpu.VMEM(halos, jnp.bfloat16),
            pltpu.VMEM(halos, jnp.bfloat16),
            pltpu.VMEM(halos, jnp.bfloat16),
            pltpu.VMEM((COLS, COLS), jnp.float32),
            pltpu.VMEM((chords,) + packed, jnp.float32),
            pltpu.VMEM((spans,) + packed, jnp.float32),
            dma(flags), dma(flags), dma(flags), dma(flags),
            dma((chords,)), dma((chords,)), dma((spans,)), dma((spans,)),
        ],
        compiler_params=pltpu.CompilerParams(
            collective_id=0, has_side_effects=True, vmem_limit_bytes=62 * 1024 * 1024
        ),
        name="filters",
    )(start_block, blocks, blk_col, block_scale)


def solution(mesh):
    in_specs = (
        P(None, ("span", "chord")),
        P(("span", "chord"), None, None),
        P(("span", "chord")),
        P(("span", "chord")),
    )
    out_specs = P(None, ("span", "chord"))
    return jax.shard_map(
        functools.partial(on_device, mesh.shape["span"], mesh.shape["chord"]),
        mesh=mesh, in_specs=in_specs, out_specs=out_specs, check_vma=False,
    )
```

```python
import functools

import jax
import jax.numpy as jnp
from jax import lax
from jax.experimental import pallas as pl
from jax.experimental.pallas import tpu as pltpu
from jax.sharding import PartitionSpec as P

BS = 128
COLS = 64
BPR = 24
RB = 6
HB = 2
DEG = 3
SPREAD = 0.8
RIMS = 4
EDGE = HB * BS
OWN = RB * BS
WIDE = OWN + RIMS * EDGE
PLACES = RB + RIMS * HB
NONE = BPR
APPS = 2 * DEG
GROUPS = 2
PART = COLS // GROUPS
PAIR = 3
STRIP = COLS // 4
PANEL = 4
MESH = pl.DeviceIdType.MESH
FIRST = ((1, 0), (1, 3), (0, 1), (1, 1), (1, 2), (0, 3), (0, 0), (0, 2))
LAST = ((1, 1), (0, 3), (0, 0), (1, 3), (1, 0), (1, 2), (0, 1), (0, 2))
MIDDLE = ((1, 3), (1, 1), (1, 0), (1, 2), (0, 3), (0, 1), (0, 0), (0, 2))
NN = (((1,), (0,)), ((), ()))
NT = (((1,), (1,)), ((), ()))


def mm(a, b, dims=NN):
    return lax.dot_general(a, b, dims, preferred_element_type=jnp.float32)


def pointers(column_ref, point_ref):
    subs = lax.broadcasted_iota(jnp.int32, (8, BS), 0)
    lanes = lax.broadcasted_iota(jnp.int32, (8, BS), 1)
    own = [subs == i for i in range(RB)]
    places = []
    for n in range(BPR):
        column = jnp.zeros((8, BS), jnp.int32)
        for i in range(RB):
            column = jnp.where(own[i], column_ref[i * BPR + n], column)
        p = column
        for o in range(2, RIMS + 1):
            p = p - jnp.where(column >= o * RB, RB - HB, 0)
        places.append(p)
    mine = jnp.full((8, BS), -1, jnp.int32)
    for n in range(BPR):
        mine = jnp.where(lanes == n, places[n], mine)
    earlier = jnp.full((8, BS), NONE, jnp.int32)
    final = jnp.full((8, BS), NONE, jnp.int32)
    for n in range(BPR):
        earlier = jnp.where((mine == places[n]) & (lanes > n), n, earlier)
        final = jnp.where(lanes == places[n], n, final)
    point_ref[0] = earlier
    point_ref[1] = final


def densify(step, point_ref, scale_ref, blocks_ref, dense_ref, sums):
    half = BS // 2
    for n in range(BPR):
        for row in range(PAIR):
            i = step * PAIR + row
            earlier = point_ref[0, i, n]
            scale = scale_ref[i * BPR + n]
            for h in range(2):
                block = blocks_ref[i * BPR + n, h * half : (h + 1) * half, :]
                partial = sums[2 * row + h]
                partial[n] = partial[earlier] + block.astype(jnp.float32) * scale
    for row in range(PAIR):
        i = step * PAIR + row
        for p in range(PLACES):
            final = point_ref[1, i, p]
            for h in range(2):
                top = i * BS + h * half
                dense_ref[top : top + half, p * BS : (p + 1) * BS] = sums[2 * row + h][final].astype(jnp.bfloat16)


def inverse_factor(gram):
    rows = lax.broadcasted_iota(jnp.int32, (COLS, COLS), 0)
    cols = lax.broadcasted_iota(jnp.int32, (COLS, COLS), 1)
    eye = (rows == cols).astype(jnp.float32)
    work = jnp.concatenate([gram, eye], axis=1)
    index = lax.broadcasted_iota(jnp.int32, (COLS, 2 * COLS), 0)
    done = []
    for start in range(0, COLS, PANEL):
        base = start // 8 * 8
        if start % 8 == 0 and start:
            done.append(work[:8])
            work = work[8:]
        panel = [jnp.broadcast_to(work[:, k : k + 1], work.shape) for k in range(start, start + PANEL)]
        for j in range(PANEL):
            at = start + j - base
            scale = 1.0 / panel[j][at : at + 1]
            factor = jnp.where(index[base:] > start + j, panel[j], 0.0)
            for later in range(j + 1, PANEL):
                panel[later] = panel[later] - factor * (panel[later][at : at + 1] * scale)
            work = work - factor * (work[at : at + 1] * scale)
    done.append(work)
    work = jnp.concatenate(done, axis=0)
    diagonal = jnp.sum(jnp.where(rows == cols, work[:, :COLS], 0.0), axis=1, keepdims=True)
    return work[:, COLS:] / jnp.sqrt(diagonal)


def halves(values):
    high = values.astype(jnp.bfloat16)
    return high, (values - high.astype(jnp.float32)).astype(jnp.bfloat16)


def pack(gram):
    rows = [gram[i * STRIP : (i + 1) * STRIP, i * STRIP :] for i in range(4)]
    quarter = STRIP // 4
    return jnp.concatenate(
        [
            jnp.concatenate([rows[0], rows[1], rows[3]], axis=1),
            jnp.concatenate([rows[2][j * quarter : (j + 1) * quarter] for j in range(4)], axis=1),
        ],
        axis=0,
    )


def unpack(packed):
    top, tail = packed[:STRIP], packed[STRIP:]
    wide = 2 * STRIP
    rows = [
        top[:, :COLS],
        top[:, COLS : 2 * COLS - STRIP],
        jnp.concatenate([tail[:, j * wide : (j + 1) * wide] for j in range(4)], axis=0),
        top[:, 2 * COLS - STRIP :],
    ]
    upper = jnp.concatenate(
        [rows[0]]
        + [jnp.concatenate([jnp.zeros((STRIP, i * STRIP), jnp.float32), rows[i]], axis=1) for i in range(1, 4)],
        axis=0,
    )
    down = lax.broadcasted_iota(jnp.int32, (COLS, COLS), 0) // STRIP
    right = lax.broadcasted_iota(jnp.int32, (COLS, COLS), 1) // STRIP
    return jnp.where(right >= down, upper, upper.T)


def filters(
    spans, chords,
    start_hbm, blocks_hbm, column_hbm, scale_hbm, out_ref,
    start_ref, start_sem, blocks_ref, blocks_sem, column_ref, column_sem, scale_ref, scale_sem,
    lanes_ref, point_ref, point_sem, sums_a, sums_b, sums_c, sums_d, sums_e, sums_f,
    dense_ref, across, mutual, prev, cur, total, edge, given, rims, back, inverse,
    chord_parts, span_parts,
    edge_send, edge_recv, back_send, back_recv,
    chord_send, chord_recv, span_send, span_recv,
):
    s = lax.axis_index("span")
    c = lax.axis_index("chord")
    after = lax.rem(c + 1, chords)
    before = lax.rem(c + chords - 1, chords)
    last = spans - 1

    barrier = pltpu.get_barrier_semaphore()

    def greet(a, b):
        pl.semaphore_signal(barrier, inc=1, device_id=(a, b), device_id_type=MESH)

    @pl.when(s > 0)
    def _():
        greet(s - 1, before)
        greet(s - 1, after)

    @pl.when(s < last)
    def _():
        greet(s + 1, before)
        greet(s + 1, after)

    for step in (1, chords - 1, *range(2, chords - 1)):
        greet(s, lax.rem(c + step, chords))
    for step in (1, spans - 1, *range(2, spans - 1)):
        greet(lax.rem(s + step, spans), c)

    columns = pltpu.make_async_copy(column_hbm, column_ref, column_sem)
    columns.start()
    scales = pltpu.make_async_copy(scale_hbm, scale_ref, scale_sem)
    scales.start()
    chunk = PAIR * BPR
    fetches = [
        pltpu.make_async_copy(
            blocks_hbm.at[q * chunk : (q + 1) * chunk], blocks_ref.at[q * chunk : (q + 1) * chunk], blocks_sem.at[q]
        )
        for q in range(RB // PAIR)
    ]
    for fetch in fetches:
        fetch.start()
    begin = pltpu.make_async_copy(start_hbm, start_ref, start_sem)
    begin.start()

    columns.wait()
    pointers(column_ref, lanes_ref)
    move = pltpu.make_async_copy(lanes_ref, point_ref, point_sem)
    move.start()
    sums = (sums_a, sums_b, sums_c, sums_d, sums_e, sums_f)
    for partial in sums:
        partial[NONE] = jnp.zeros(partial.shape[1:], jnp.float32)

    @pl.when(s == last)
    def _():
        rims[:, :, 1:] = jnp.zeros(rims[:, :, 1:].shape, rims.dtype)

    @pl.when(s == 0)
    def _():
        back[:, :, 1:] = jnp.zeros(back[:, :, 1:].shape, back.dtype)

    prev[...] = jnp.zeros_like(prev)
    scales.wait()
    move.wait()
    for q in range(RB // PAIR):
        fetches[q].wait()
        densify(q, point_ref, scale_ref, blocks_ref, dense_ref, sums)
    begin.wait()
    for g in range(GROUPS):
        cur[g] = start_ref[g * PART : (g + 1) * PART, :]
    corners = 2 * (jnp.minimum(s, 1) + jnp.minimum(last - s, 1))
    down = jnp.maximum(s - 1, 0)
    up = jnp.minimum(s + 1, last)
    edge_to = [(s, before), (down, after), (down, c), (down, before)]
    back_to = [(s, after), (up, before), (up, c), (up, after)]

    def edge_copy(k, g, o):
        return pltpu.make_async_remote_copy(
            src_ref=edge.at[k, g], dst_ref=rims.at[k, g, o],
            send_sem=edge_send.at[k, g, o], recv_sem=edge_recv.at[k, g, o],
            device_id=edge_to[o], device_id_type=MESH,
        )

    def back_copy(k, g, o):
        return pltpu.make_async_remote_copy(
            src_ref=given.at[k, g, o], dst_ref=back.at[k, g, o],
            send_sem=back_send.at[k, g, o], recv_sem=back_recv.at[k, g, o],
            device_id=back_to[o], device_id_type=MESH,
        )

    def chord_copy(step):
        return pltpu.make_async_remote_copy(
            src_ref=chord_parts.at[c], dst_ref=chord_parts.at[c],
            send_sem=chord_send.at[step], recv_sem=chord_recv.at[step],
            device_id=(s, lax.rem(c + step, chords)), device_id_type=MESH,
        )

    def span_copy(step):
        return pltpu.make_async_remote_copy(
            src_ref=span_parts.at[s], dst_ref=span_parts.at[s],
            send_sem=span_send.at[step], recv_sem=span_recv.at[step],
            device_id=(lax.rem(s + step, spans), c), device_id_type=MESH,
        )

    def halo(o, inner, outer):
        if o == 0:
            inner()
        else:
            pl.when(outer)(inner)

    def rim_dense(o):
        return dense_ref[:, OWN + o * EDGE : OWN + (o + 1) * EDGE]

    def give(k, g, o, narrowed):
        given[k, g, o] = mm(narrowed, rim_dense(o)).astype(jnp.bfloat16)

    def send(k, g, ready=False):
        if not ready:
            edge[k, g] = cur[g, :, :EDGE].astype(jnp.bfloat16)
        narrowed = cur[g].astype(jnp.bfloat16)

        def issue(steps):
            for out, o in steps:
                if out:
                    halo(o, lambda o=o: edge_copy(k, g, o).start(), s > 0)
                else:
                    if not ready:
                        give(k, g, o, narrowed)
                    halo(o, lambda o=o: back_copy(k, g, o).start(), s < last)

        pl.when(c == 0)(lambda: issue(FIRST))
        pl.when(c == chords - 1)(lambda: issue(LAST))
        pl.when((c > 0) & (c < chords - 1))(lambda: issue(MIDDLE))
        if isinstance(k, int):
            for q in range(RB // HB):
                lo, hi = q * EDGE, (q + 1) * EDGE
                total[g, :, lo:hi] = mm(narrowed[:, :hi], dense_ref[:hi, lo:hi]) + mm(
                    narrowed[:, lo:], dense_ref[lo:hi, lo:OWN], NT
                )
        else:
            total[g] = mm(narrowed, mutual[...])

    def receive(k, g):

        def gather(first_part, rest):
            for part in (first_part, rest):
                for o in part:
                    halo(o, lambda o=o: edge_copy(k, g, o).wait_recv(), s < last)
                acc = total[g]
                for o in part:
                    acc = acc + mm(rims[k, g, o], across[o * EDGE : (o + 1) * EDGE, :])
                total[g] = acc

        pl.when(c == 0)(lambda: gather((2, 0, 3), (1,)))
        pl.when(c > 0)(lambda: gather((2, 1), (0, 3)))
        applied = total[g]
        for o in (2, 0, 1, 3):
            halo(o, lambda o=o: back_copy(k, g, o).wait_recv(), s > 0)
        returned = back[k, g, 0].astype(jnp.float32)
        for o in range(1, RIMS):
            returned = returned + back[k, g, o].astype(jnp.float32)
        applied = jnp.concatenate([applied[:, :EDGE] + returned, applied[:, EDGE:]], axis=1)
        first = lax.rem(k, DEG) == 0
        gain = jnp.where(first, 1.0 / SPREAD, 2.0 / SPREAD)
        keep = jnp.where(first, 0.0, 1.0)
        following = applied * gain - prev[g] * keep
        prev[g] = cur[g]
        cur[g] = following

    narrowed = cur[0].astype(jnp.bfloat16)
    edge[0, 0] = narrowed[:, :EDGE]
    for o in range(RIMS):
        give(0, 0, o, narrowed)
    pl.semaphore_wait(barrier, chords - 1 + spans - 1 + corners)
    for g in range(GROUPS):
        send(0, g, ready=g == 0)

    rows = lax.broadcasted_iota(jnp.int32, (EDGE, EDGE), 0)
    cols = lax.broadcasted_iota(jnp.int32, (EDGE, EDGE), 1)
    eye = (rows == cols).astype(jnp.bfloat16)
    for o in range(RIMS):
        across[o * EDGE : (o + 1) * EDGE, :] = mm(eye, rim_dense(o), NT).astype(jnp.bfloat16)
    for q in range(RB // HB):
        lo, hi = q * EDGE, (q + 1) * EDGE
        turned = mm(eye, dense_ref[:, lo:hi], NT)
        mutual[lo:hi, :] = (dense_ref[lo:hi, :OWN].astype(jnp.float32) + turned).astype(jnp.bfloat16)

    def drain(k):
        for g in range(GROUPS):
            for o in range(RIMS):
                halo(o, lambda o=o: edge_copy(k, g, o).wait_send(), s > 0)
                halo(o, lambda o=o: back_copy(k, g, o).wait_send(), s < last)

    def advance(k, carry):
        for g in range(GROUPS):
            receive(k - 1, g)
            send(k, g)

        @pl.when(k == DEG)
        def _():
            basis = cur[...].reshape(COLS, OWN)
            high, low = halves(basis)
            both = mm(jnp.concatenate([high, low], axis=0), high, NT)
            gram = both[:COLS] + both[COLS:] + both[COLS:].T
            chord_parts[c] = pack(gram)
            for step in range(1, chords):
                chord_copy(step).start()

        @pl.when(k == DEG + 1)
        def _():
            for step in range(1, chords):
                chord_copy(step).wait_recv()
            part = chord_parts[0]
            for step in range(1, chords):
                part = part + chord_parts[step]
            span_parts[s] = part
            for step in range(1, spans):
                span_copy(step).start()

        @pl.when(k == DEG + 2)
        def _():
            for step in range(1, spans):
                span_copy(step).wait_recv()
            part = span_parts[0]
            for step in range(1, spans):
                part = part + span_parts[step]
            part = part / float(OWN * spans * chords)
            inverse[...] = inverse_factor(unpack(part))

        drain(k - 1)
        return carry

    lax.fori_loop(1, APPS, advance, 0)
    receive(jnp.int32(APPS - 1), 0)
    drain(APPS - 1)
    for step in range(1, chords):
        chord_copy(step).wait_send()
    for step in range(1, spans):
        span_copy(step).wait_send()
    receive(jnp.int32(APPS - 1), 1)
    left, right = halves(inverse[...]), halves(cur[...].reshape(COLS, OWN))
    out_ref[...] = mm(
        jnp.concatenate([left[0], left[0], left[1]], axis=1), jnp.concatenate([right[0], right[1], right[0]], axis=0)
    )


def on_device(spans, chords, start_block, blocks, blk_col, block_scale):
    vmem = pl.BlockSpec(memory_space=pltpu.VMEM)
    dma = pltpu.SemaphoreType.DMA
    packed = (STRIP + STRIP // 4, 2 * COLS)
    split = (GROUPS, PART, OWN)
    flags = (APPS, GROUPS, RIMS)
    halos = flags + (PART, EDGE)
    return pl.pallas_call(
        functools.partial(filters, spans, chords),
        out_shape=jax.ShapeDtypeStruct((COLS, OWN), jnp.float32),
        in_specs=[pl.BlockSpec(memory_space=pl.ANY)] * 4,
        out_specs=vmem,
        scratch_shapes=[
            pltpu.VMEM((COLS, OWN), jnp.float32),
            dma,
            pltpu.VMEM(blocks.shape, jnp.bfloat16),
            dma((RB // PAIR,)),
            pltpu.SMEM(blk_col.shape, jnp.int32),
            dma,
            pltpu.SMEM(block_scale.shape, jnp.float32),
            dma,
            pltpu.VMEM((2, 8, BS), jnp.int32),
            pltpu.SMEM((2, 8, BS), jnp.int32),
            dma,
            *[pltpu.VMEM((BPR + 1, BS // 2, BS), jnp.float32)] * (2 * PAIR),
            pltpu.VMEM((OWN, WIDE), jnp.bfloat16),
            pltpu.VMEM((RIMS * EDGE, OWN), jnp.bfloat16),
            pltpu.VMEM((OWN, OWN), jnp.bfloat16),
            pltpu.VMEM(split, jnp.float32),
            pltpu.VMEM(split, jnp.float32),
            pltpu.VMEM(split, jnp.float32),
            pltpu.VMEM((APPS, GROUPS, PART, EDGE), jnp.bfloat16),
            pltpu.VMEM(halos, jnp.bfloat16),
            pltpu.VMEM(halos, jnp.bfloat16),
            pltpu.VMEM(halos, jnp.bfloat16),
            pltpu.VMEM((COLS, COLS), jnp.float32),
            pltpu.VMEM((chords,) + packed, jnp.float32),
            pltpu.VMEM((spans,) + packed, jnp.float32),
            dma(flags), dma(flags), dma(flags), dma(flags),
            dma((chords,)), dma((chords,)), dma((spans,)), dma((spans,)),
        ],
        compiler_params=pltpu.CompilerParams(
            collective_id=0, has_side_effects=True, vmem_limit_bytes=62 * 1024 * 1024
        ),
        name="filters",
    )(start_block, blocks, blk_col, block_scale)


def solution(mesh):
    in_specs = (
        P(None, ("span", "chord")),
        P(("span", "chord"), None, None),
        P(("span", "chord")),
        P(("span", "chord")),
    )
    out_specs = P(None, ("span", "chord"))
    return jax.shard_map(
        functools.partial(on_device, mesh.shape["span"], mesh.shape["chord"]),
        mesh=mesh, in_specs=in_specs, out_specs=out_specs, check_vma=False,
    )
```

```python
import functools

import jax
import jax.numpy as jnp
from jax import lax
from jax.experimental import pallas as pl
from jax.experimental.pallas import tpu as pltpu
from jax.sharding import PartitionSpec as P

BS = 128
COLS = 64
BPR = 24
RB = 6
HB = 2
DEG = 3
SPREAD = 0.8
RIMS = 4
EDGE = HB * BS
OWN = RB * BS
WIDE = OWN + RIMS * EDGE
PLACES = RB + RIMS * HB
NONE = BPR
APPS = 2 * DEG
GROUPS = 2
PART = COLS // GROUPS
PAIR = 3
STRIP = COLS // 4
PANEL = 4
MESH = pl.DeviceIdType.MESH
FIRST = ((1, 3), (1, 0), (0, 1), (1, 1), (1, 2), (0, 3), (0, 0), (0, 2))
LAST = ((1, 1), (0, 3), (0, 0), (1, 3), (1, 0), (1, 2), (0, 1), (0, 2))
MIDDLE = ((1, 3), (1, 1), (1, 0), (1, 2), (0, 3), (0, 1), (0, 0), (0, 2))
NN = (((1,), (0,)), ((), ()))
NT = (((1,), (1,)), ((), ()))


def mm(a, b, dims=NN):
    return lax.dot_general(a, b, dims, preferred_element_type=jnp.float32)


def pointers(column_ref, point_ref):
    subs = lax.broadcasted_iota(jnp.int32, (8, BS), 0)
    lanes = lax.broadcasted_iota(jnp.int32, (8, BS), 1)
    own = [subs == i for i in range(RB)]
    places = []
    for n in range(BPR):
        column = jnp.zeros((8, BS), jnp.int32)
        for i in range(RB):
            column = jnp.where(own[i], column_ref[i * BPR + n], column)
        p = column
        for o in range(2, RIMS + 1):
            p = p - jnp.where(column >= o * RB, RB - HB, 0)
        places.append(p)
    mine = jnp.full((8, BS), -1, jnp.int32)
    for n in range(BPR):
        mine = jnp.where(lanes == n, places[n], mine)
    earlier = jnp.full((8, BS), NONE, jnp.int32)
    final = jnp.full((8, BS), NONE, jnp.int32)
    for n in range(BPR):
        earlier = jnp.where((mine == places[n]) & (lanes > n), n, earlier)
        final = jnp.where(lanes == places[n], n, final)
    point_ref[0] = earlier
    point_ref[1] = final


def densify(step, point_ref, scale_ref, blocks_ref, dense_ref, sums):
    half = BS // 2
    for n in range(BPR):
        for row in range(PAIR):
            i = step * PAIR + row
            earlier = point_ref[0, i, n]
            scale = scale_ref[i * BPR + n]
            for h in range(2):
                block = blocks_ref[i * BPR + n, h * half : (h + 1) * half, :]
                partial = sums[2 * row + h]
                partial[n] = partial[earlier] + block.astype(jnp.float32) * scale
    for row in range(PAIR):
        i = step * PAIR + row
        for p in range(PLACES):
            final = point_ref[1, i, p]
            for h in range(2):
                top = i * BS + h * half
                dense_ref[top : top + half, p * BS : (p + 1) * BS] = sums[2 * row + h][final].astype(jnp.bfloat16)


def inverse_factor(gram):
    rows = lax.broadcasted_iota(jnp.int32, (COLS, COLS), 0)
    cols = lax.broadcasted_iota(jnp.int32, (COLS, COLS), 1)
    eye = (rows == cols).astype(jnp.float32)
    work = jnp.concatenate([gram, eye], axis=1)
    index = lax.broadcasted_iota(jnp.int32, (COLS, 2 * COLS), 0)
    done = []
    for start in range(0, COLS, PANEL):
        base = start // 8 * 8
        if start % 8 == 0 and start:
            done.append(work[:8])
            work = work[8:]
        panel = [jnp.broadcast_to(work[:, k : k + 1], work.shape) for k in range(start, start + PANEL)]
        for j in range(PANEL):
            at = start + j - base
            scale = 1.0 / panel[j][at : at + 1]
            factor = jnp.where(index[base:] > start + j, panel[j], 0.0)
            for later in range(j + 1, PANEL):
                panel[later] = panel[later] - factor * (panel[later][at : at + 1] * scale)
            work = work - factor * (work[at : at + 1] * scale)
    done.append(work)
    work = jnp.concatenate(done, axis=0)
    diagonal = jnp.sum(jnp.where(rows == cols, work[:, :COLS], 0.0), axis=1, keepdims=True)
    return work[:, COLS:] / jnp.sqrt(diagonal)


def halves(values):
    high = values.astype(jnp.bfloat16)
    return high, (values - high.astype(jnp.float32)).astype(jnp.bfloat16)


def pack(gram):
    rows = [gram[i * STRIP : (i + 1) * STRIP, i * STRIP :] for i in range(4)]
    quarter = STRIP // 4
    return jnp.concatenate(
        [
            jnp.concatenate([rows[0], rows[1], rows[3]], axis=1),
            jnp.concatenate([rows[2][j * quarter : (j + 1) * quarter] for j in range(4)], axis=1),
        ],
        axis=0,
    )


def unpack(packed):
    top, tail = packed[:STRIP], packed[STRIP:]
    wide = 2 * STRIP
    rows = [
        top[:, :COLS],
        top[:, COLS : 2 * COLS - STRIP],
        jnp.concatenate([tail[:, j * wide : (j + 1) * wide] for j in range(4)], axis=0),
        top[:, 2 * COLS - STRIP :],
    ]
    upper = jnp.concatenate(
        [rows[0]]
        + [jnp.concatenate([jnp.zeros((STRIP, i * STRIP), jnp.float32), rows[i]], axis=1) for i in range(1, 4)],
        axis=0,
    )
    down = lax.broadcasted_iota(jnp.int32, (COLS, COLS), 0) // STRIP
    right = lax.broadcasted_iota(jnp.int32, (COLS, COLS), 1) // STRIP
    return jnp.where(right >= down, upper, upper.T)


def filters(
    spans, chords,
    start_hbm, blocks_hbm, column_hbm, scale_hbm, out_ref,
    start_ref, start_sem, blocks_ref, blocks_sem, column_ref, column_sem, scale_ref, scale_sem,
    lanes_ref, point_ref, point_sem, sums_a, sums_b, sums_c, sums_d, sums_e, sums_f,
    dense_ref, across, mutual, prev, cur, total, edge, given, rims, back, inverse,
    chord_parts, span_parts,
    edge_send, edge_recv, back_send, back_recv,
    chord_send, chord_recv, span_send, span_recv,
):
    s = lax.axis_index("span")
    c = lax.axis_index("chord")
    after = lax.rem(c + 1, chords)
    before = lax.rem(c + chords - 1, chords)
    last = spans - 1

    barrier = pltpu.get_barrier_semaphore()

    def greet(a, b):
        pl.semaphore_signal(barrier, inc=1, device_id=(a, b), device_id_type=MESH)

    @pl.when(s > 0)
    def _():
        greet(s - 1, before)
        greet(s - 1, after)

    @pl.when(s < last)
    def _():
        greet(s + 1, before)
        greet(s + 1, after)

    for step in (1, chords - 1, *range(2, chords - 1)):
        greet(s, lax.rem(c + step, chords))
    for step in (1, spans - 1, *range(2, spans - 1)):
        greet(lax.rem(s + step, spans), c)

    columns = pltpu.make_async_copy(column_hbm, column_ref, column_sem)
    columns.start()
    scales = pltpu.make_async_copy(scale_hbm, scale_ref, scale_sem)
    scales.start()
    chunk = PAIR * BPR
    fetches = [
        pltpu.make_async_copy(
            blocks_hbm.at[q * chunk : (q + 1) * chunk], blocks_ref.at[q * chunk : (q + 1) * chunk], blocks_sem.at[q]
        )
        for q in range(RB // PAIR)
    ]
    for fetch in fetches:
        fetch.start()
    begin = pltpu.make_async_copy(start_hbm, start_ref, start_sem)
    begin.start()

    columns.wait()
    pointers(column_ref, lanes_ref)
    move = pltpu.make_async_copy(lanes_ref, point_ref, point_sem)
    move.start()
    sums = (sums_a, sums_b, sums_c, sums_d, sums_e, sums_f)
    for partial in sums:
        partial[NONE] = jnp.zeros(partial.shape[1:], jnp.float32)

    @pl.when(s == last)
    def _():
        rims[:, :, 1:] = jnp.zeros(rims[:, :, 1:].shape, rims.dtype)

    @pl.when(s == 0)
    def _():
        back[:, :, 1:] = jnp.zeros(back[:, :, 1:].shape, back.dtype)

    prev[...] = jnp.zeros_like(prev)
    scales.wait()
    move.wait()
    for q in range(RB // PAIR):
        fetches[q].wait()
        densify(q, point_ref, scale_ref, blocks_ref, dense_ref, sums)
    begin.wait()
    for g in range(GROUPS):
        cur[g] = start_ref[g * PART : (g + 1) * PART, :]
    corners = 2 * (jnp.minimum(s, 1) + jnp.minimum(last - s, 1))
    down = jnp.maximum(s - 1, 0)
    up = jnp.minimum(s + 1, last)
    edge_to = [(s, before), (down, after), (down, c), (down, before)]
    back_to = [(s, after), (up, before), (up, c), (up, after)]

    def edge_copy(k, g, o):
        return pltpu.make_async_remote_copy(
            src_ref=edge.at[k, g], dst_ref=rims.at[k, g, o],
            send_sem=edge_send.at[k, g, o], recv_sem=edge_recv.at[k, g, o],
            device_id=edge_to[o], device_id_type=MESH,
        )

    def back_copy(k, g, o):
        return pltpu.make_async_remote_copy(
            src_ref=given.at[k, g, o], dst_ref=back.at[k, g, o],
            send_sem=back_send.at[k, g, o], recv_sem=back_recv.at[k, g, o],
            device_id=back_to[o], device_id_type=MESH,
        )

    def chord_copy(step):
        return pltpu.make_async_remote_copy(
            src_ref=chord_parts.at[c], dst_ref=chord_parts.at[c],
            send_sem=chord_send.at[step], recv_sem=chord_recv.at[step],
            device_id=(s, lax.rem(c + step, chords)), device_id_type=MESH,
        )

    def span_copy(step):
        return pltpu.make_async_remote_copy(
            src_ref=span_parts.at[s], dst_ref=span_parts.at[s],
            send_sem=span_send.at[step], recv_sem=span_recv.at[step],
            device_id=(lax.rem(s + step, spans), c), device_id_type=MESH,
        )

    def halo(o, inner, outer):
        if o == 0:
            inner()
        else:
            pl.when(outer)(inner)

    def rim_dense(o):
        return dense_ref[:, OWN + o * EDGE : OWN + (o + 1) * EDGE]

    def give(k, g, o, narrowed):
        given[k, g, o] = mm(narrowed, rim_dense(o)).astype(jnp.bfloat16)

    def send(k, g, ready=False):
        if not ready:
            edge[k, g] = cur[g, :, :EDGE].astype(jnp.bfloat16)
        narrowed = cur[g].astype(jnp.bfloat16)

        def issue(steps):
            for out, o in steps:
                if out:
                    halo(o, lambda o=o: edge_copy(k, g, o).start(), s > 0)
                else:
                    if not ready:
                        give(k, g, o, narrowed)
                    halo(o, lambda o=o: back_copy(k, g, o).start(), s < last)

        pl.when(c == 0)(lambda: issue(FIRST))
        pl.when(c == chords - 1)(lambda: issue(LAST))
        pl.when((c > 0) & (c < chords - 1))(lambda: issue(MIDDLE))
        if isinstance(k, int):
            for q in range(RB // HB):
                lo, hi = q * EDGE, (q + 1) * EDGE
                total[g, :, lo:hi] = mm(narrowed[:, :hi], dense_ref[:hi, lo:hi]) + mm(
                    narrowed[:, lo:], dense_ref[lo:hi, lo:OWN], NT
                )
        else:
            total[g] = mm(narrowed, mutual[...])

    def receive(k, g):

        def gather(first_part, rest):
            for part in (first_part, rest):
                for o in part:
                    halo(o, lambda o=o: edge_copy(k, g, o).wait_recv(), s < last)
                acc = total[g]
                for o in part:
                    acc = acc + mm(rims[k, g, o], across[o * EDGE : (o + 1) * EDGE, :])
                total[g] = acc

        pl.when(c == 0)(lambda: gather((2, 0, 3), (1,)))
        pl.when(c > 0)(lambda: gather((2, 1), (0, 3)))
        applied = total[g]
        for o in (2, 0, 1, 3):
            halo(o, lambda o=o: back_copy(k, g, o).wait_recv(), s > 0)
        returned = back[k, g, 0].astype(jnp.float32)
        for o in range(1, RIMS):
            returned = returned + back[k, g, o].astype(jnp.float32)
        applied = jnp.concatenate([applied[:, :EDGE] + returned, applied[:, EDGE:]], axis=1)
        first = lax.rem(k, DEG) == 0
        gain = jnp.where(first, 1.0 / SPREAD, 2.0 / SPREAD)
        keep = jnp.where(first, 0.0, 1.0)
        following = applied * gain - prev[g] * keep
        prev[g] = cur[g]
        cur[g] = following

    narrowed = cur[0].astype(jnp.bfloat16)
    edge[0, 0] = narrowed[:, :EDGE]
    for o in range(RIMS):
        give(0, 0, o, narrowed)
    pl.semaphore_wait(barrier, chords - 1 + spans - 1 + corners)
    for g in range(GROUPS):
        send(0, g, ready=g == 0)

    rows = lax.broadcasted_iota(jnp.int32, (EDGE, EDGE), 0)
    cols = lax.broadcasted_iota(jnp.int32, (EDGE, EDGE), 1)
    eye = (rows == cols).astype(jnp.bfloat16)
    for o in range(RIMS):
        across[o * EDGE : (o + 1) * EDGE, :] = mm(eye, rim_dense(o), NT).astype(jnp.bfloat16)
    for q in range(RB // HB):
        lo, hi = q * EDGE, (q + 1) * EDGE
        turned = mm(eye, dense_ref[:, lo:hi], NT)
        mutual[lo:hi, :] = (dense_ref[lo:hi, :OWN].astype(jnp.float32) + turned).astype(jnp.bfloat16)

    def drain(k):
        for g in range(GROUPS):
            for o in range(RIMS):
                halo(o, lambda o=o: edge_copy(k, g, o).wait_send(), s > 0)
                halo(o, lambda o=o: back_copy(k, g, o).wait_send(), s < last)

    def advance(k, carry):
        for g in range(GROUPS):
            receive(k - 1, g)
            send(k, g)

        @pl.when(k == DEG)
        def _():
            basis = cur[...].reshape(COLS, OWN)
            high, low = halves(basis)
            both = mm(jnp.concatenate([high, low], axis=0), high, NT)
            gram = both[:COLS] + both[COLS:] + both[COLS:].T
            chord_parts[c] = pack(gram)
            for step in range(1, chords):
                chord_copy(step).start()

        @pl.when(k == DEG + 1)
        def _():
            for step in range(1, chords):
                chord_copy(step).wait_recv()
            part = chord_parts[0]
            for step in range(1, chords):
                part = part + chord_parts[step]
            span_parts[s] = part
            for step in range(1, spans):
                span_copy(step).start()

        @pl.when(k == DEG + 2)
        def _():
            for step in range(1, spans):
                span_copy(step).wait_recv()
            part = span_parts[0]
            for step in range(1, spans):
                part = part + span_parts[step]
            part = part / float(OWN * spans * chords)
            inverse[...] = inverse_factor(unpack(part))

        drain(k - 1)
        return carry

    lax.fori_loop(1, APPS, advance, 0)
    receive(jnp.int32(APPS - 1), 0)
    drain(APPS - 1)
    for step in range(1, chords):
        chord_copy(step).wait_send()
    for step in range(1, spans):
        span_copy(step).wait_send()
    receive(jnp.int32(APPS - 1), 1)
    left, right = halves(inverse[...]), halves(cur[...].reshape(COLS, OWN))
    out_ref[...] = mm(
        jnp.concatenate([left[0], left[0], left[1]], axis=1), jnp.concatenate([right[0], right[1], right[0]], axis=0)
    )


def on_device(spans, chords, start_block, blocks, blk_col, block_scale):
    vmem = pl.BlockSpec(memory_space=pltpu.VMEM)
    dma = pltpu.SemaphoreType.DMA
    packed = (STRIP + STRIP // 4, 2 * COLS)
    split = (GROUPS, PART, OWN)
    flags = (APPS, GROUPS, RIMS)
    halos = flags + (PART, EDGE)
    return pl.pallas_call(
        functools.partial(filters, spans, chords),
        out_shape=jax.ShapeDtypeStruct((COLS, OWN), jnp.float32),
        in_specs=[pl.BlockSpec(memory_space=pl.ANY)] * 4,
        out_specs=vmem,
        scratch_shapes=[
            pltpu.VMEM((COLS, OWN), jnp.float32),
            dma,
            pltpu.VMEM(blocks.shape, jnp.bfloat16),
            dma((RB // PAIR,)),
            pltpu.SMEM(blk_col.shape, jnp.int32),
            dma,
            pltpu.SMEM(block_scale.shape, jnp.float32),
            dma,
            pltpu.VMEM((2, 8, BS), jnp.int32),
            pltpu.SMEM((2, 8, BS), jnp.int32),
            dma,
            *[pltpu.VMEM((BPR + 1, BS // 2, BS), jnp.float32)] * (2 * PAIR),
            pltpu.VMEM((OWN, WIDE), jnp.bfloat16),
            pltpu.VMEM((RIMS * EDGE, OWN), jnp.bfloat16),
            pltpu.VMEM((OWN, OWN), jnp.bfloat16),
            pltpu.VMEM(split, jnp.float32),
            pltpu.VMEM(split, jnp.float32),
            pltpu.VMEM(split, jnp.float32),
            pltpu.VMEM((APPS, GROUPS, PART, EDGE), jnp.bfloat16),
            pltpu.VMEM(halos, jnp.bfloat16),
            pltpu.VMEM(halos, jnp.bfloat16),
            pltpu.VMEM(halos, jnp.bfloat16),
            pltpu.VMEM((COLS, COLS), jnp.float32),
            pltpu.VMEM((chords,) + packed, jnp.float32),
            pltpu.VMEM((spans,) + packed, jnp.float32),
            dma(flags), dma(flags), dma(flags), dma(flags),
            dma((chords,)), dma((chords,)), dma((spans,)), dma((spans,)),
        ],
        compiler_params=pltpu.CompilerParams(
            collective_id=0, has_side_effects=True, vmem_limit_bytes=54976 * 1024
        ),
        name="filters",
    )(start_block, blocks, blk_col, block_scale)


def solution(mesh):
    in_specs = (
        P(None, ("span", "chord")),
        P(("span", "chord"), None, None),
        P(("span", "chord")),
        P(("span", "chord")),
    )
    out_specs = P(None, ("span", "chord"))
    return jax.shard_map(
        functools.partial(on_device, mesh.shape["span"], mesh.shape["chord"]),
        mesh=mesh, in_specs=in_specs, out_specs=out_specs, check_vma=False,
    )
```

```python
import functools

import jax
import jax.numpy as jnp
from jax import lax
from jax.experimental import pallas as pl
from jax.experimental.pallas import tpu as pltpu
from jax.sharding import PartitionSpec as P

BS = 128
COLS = 64
BPR = 24
RB = 6
HB = 2
DEG = 3
SPREAD = 0.8
RIMS = 4
EDGE = HB * BS
OWN = RB * BS
WIDE = OWN + RIMS * EDGE
PLACES = RB + RIMS * HB
NONE = BPR
APPS = 2 * DEG
GROUPS = 2
PART = COLS // GROUPS
PAIR = 3
STRIP = COLS // 4
PANEL = 4
MESH = pl.DeviceIdType.MESH
FIRST = ((1, 3), (1, 0), (0, 1), (1, 1), (1, 2), (0, 3), (0, 0), (0, 2))
LAST = ((1, 1), (0, 3), (0, 0), (1, 3), (1, 0), (1, 2), (0, 1), (0, 2))
MIDDLE = ((1, 3), (1, 1), (1, 0), (1, 2), (0, 3), (0, 1), (0, 0), (0, 2))
NN = (((1,), (0,)), ((), ()))
NT = (((1,), (1,)), ((), ()))


def mm(a, b, dims=NN):
    return lax.dot_general(a, b, dims, preferred_element_type=jnp.float32)


def pointers(column_ref, point_ref):
    subs = lax.broadcasted_iota(jnp.int32, (8, BS), 0)
    lanes = lax.broadcasted_iota(jnp.int32, (8, BS), 1)
    own = [subs == i for i in range(RB)]
    places = []
    for n in range(BPR):
        column = jnp.zeros((8, BS), jnp.int32)
        for i in range(RB):
            column = jnp.where(own[i], column_ref[i * BPR + n], column)
        p = column
        for o in range(2, RIMS + 1):
            p = p - jnp.where(column >= o * RB, RB - HB, 0)
        places.append(p)
    mine = jnp.full((8, BS), -1, jnp.int32)
    for n in range(BPR):
        mine = jnp.where(lanes == n, places[n], mine)
    earlier = jnp.full((8, BS), NONE, jnp.int32)
    final = jnp.full((8, BS), NONE, jnp.int32)
    for n in range(BPR):
        earlier = jnp.where((mine == places[n]) & (lanes > n), n, earlier)
        final = jnp.where(lanes == places[n], n, final)
    point_ref[0] = earlier
    point_ref[1] = final


def densify(step, point_ref, scale_ref, blocks_ref, dense_ref, sums):
    half = BS // 2
    for n in range(BPR):
        for row in range(PAIR):
            i = step * PAIR + row
            earlier = point_ref[0, i, n]
            scale = scale_ref[i * BPR + n]
            for h in range(2):
                block = blocks_ref[i * BPR + n, h * half : (h + 1) * half, :]
                partial = sums[2 * row + h]
                partial[n] = partial[earlier] + block.astype(jnp.float32) * scale
    for row in range(PAIR):
        i = step * PAIR + row
        for p in range(PLACES):
            final = point_ref[1, i, p]
            for h in range(2):
                top = i * BS + h * half
                dense_ref[top : top + half, p * BS : (p + 1) * BS] = sums[2 * row + h][final].astype(jnp.bfloat16)


def inverse_factor(gram):
    rows = lax.broadcasted_iota(jnp.int32, (COLS, COLS), 0)
    cols = lax.broadcasted_iota(jnp.int32, (COLS, COLS), 1)
    eye = (rows == cols).astype(jnp.float32)
    work = jnp.concatenate([gram, eye], axis=1)
    index = lax.broadcasted_iota(jnp.int32, (COLS, 2 * COLS), 0)
    done = []
    for start in range(0, COLS, PANEL):
        base = start // 8 * 8
        if start % 8 == 0 and start:
            done.append(work[:8])
            work = work[8:]
        panel = [jnp.broadcast_to(work[:, k : k + 1], work.shape) for k in range(start, start + PANEL)]
        for j in range(PANEL):
            at = start + j - base
            scale = 1.0 / panel[j][at : at + 1]
            factor = jnp.where(index[base:] > start + j, panel[j], 0.0)
            for later in range(j + 1, PANEL):
                panel[later] = panel[later] - factor * (panel[later][at : at + 1] * scale)
            work = work - factor * (work[at : at + 1] * scale)
    done.append(work)
    work = jnp.concatenate(done, axis=0)
    diagonal = jnp.sum(jnp.where(rows == cols, work[:, :COLS], 0.0), axis=1, keepdims=True)
    return work[:, COLS:] / jnp.sqrt(diagonal)


def halves(values):
    high = values.astype(jnp.bfloat16)
    return high, (values - high.astype(jnp.float32)).astype(jnp.bfloat16)


def pack(gram):
    rows = [gram[i * STRIP : (i + 1) * STRIP, i * STRIP :] for i in range(4)]
    quarter = STRIP // 4
    return jnp.concatenate(
        [
            jnp.concatenate([rows[0], rows[1], rows[3]], axis=1),
            jnp.concatenate([rows[2][j * quarter : (j + 1) * quarter] for j in range(4)], axis=1),
        ],
        axis=0,
    )


def unpack(packed):
    top, tail = packed[:STRIP], packed[STRIP:]
    wide = 2 * STRIP
    rows = [
        top[:, :COLS],
        top[:, COLS : 2 * COLS - STRIP],
        jnp.concatenate([tail[:, j * wide : (j + 1) * wide] for j in range(4)], axis=0),
        top[:, 2 * COLS - STRIP :],
    ]
    upper = jnp.concatenate(
        [rows[0]]
        + [jnp.concatenate([jnp.zeros((STRIP, i * STRIP), jnp.float32), rows[i]], axis=1) for i in range(1, 4)],
        axis=0,
    )
    down = lax.broadcasted_iota(jnp.int32, (COLS, COLS), 0) // STRIP
    right = lax.broadcasted_iota(jnp.int32, (COLS, COLS), 1) // STRIP
    return jnp.where(right >= down, upper, upper.T)


def filters(
    spans, chords,
    start_hbm, blocks_hbm, column_hbm, scale_hbm, out_ref,
    start_ref, start_sem, blocks_ref, blocks_sem, column_ref, column_sem, scale_ref, scale_sem,
    lanes_ref, point_ref, point_sem, sums_a, sums_b, sums_c, sums_d, sums_e, sums_f,
    dense_ref, across, mutual, prev, cur, total, edge, given, rims, back, inverse,
    chord_parts, span_parts,
    edge_send, edge_recv, back_send, back_recv,
    chord_send, chord_recv, span_send, span_recv,
):
    s = lax.axis_index("span")
    c = lax.axis_index("chord")
    after = lax.rem(c + 1, chords)
    before = lax.rem(c + chords - 1, chords)
    last = spans - 1

    barrier = pltpu.get_barrier_semaphore()

    def greet(a, b):
        pl.semaphore_signal(barrier, inc=1, device_id=(a, b), device_id_type=MESH)

    @pl.when(s > 0)
    def _():
        greet(s - 1, before)
        greet(s - 1, after)

    @pl.when(s < last)
    def _():
        greet(s + 1, before)
        greet(s + 1, after)

    for step in (1, chords - 1, *range(2, chords - 1)):
        greet(s, lax.rem(c + step, chords))
    for step in (1, spans - 1, *range(2, spans - 1)):
        greet(lax.rem(s + step, spans), c)

    columns = pltpu.make_async_copy(column_hbm, column_ref, column_sem)
    columns.start()
    scales = pltpu.make_async_copy(scale_hbm, scale_ref, scale_sem)
    scales.start()
    chunk = PAIR * BPR
    fetches = [
        pltpu.make_async_copy(
            blocks_hbm.at[q * chunk : (q + 1) * chunk], blocks_ref.at[q * chunk : (q + 1) * chunk], blocks_sem.at[q]
        )
        for q in range(RB // PAIR)
    ]
    for fetch in fetches:
        fetch.start()
    begin = pltpu.make_async_copy(start_hbm, start_ref, start_sem)
    begin.start()

    columns.wait()
    pointers(column_ref, lanes_ref)
    move = pltpu.make_async_copy(lanes_ref, point_ref, point_sem)
    move.start()
    sums = (sums_a, sums_b, sums_c, sums_d, sums_e, sums_f)
    for partial in sums:
        partial[NONE] = jnp.zeros(partial.shape[1:], jnp.float32)

    @pl.when(s == last)
    def _():
        rims[:, :, 1:] = jnp.zeros(rims[:, :, 1:].shape, rims.dtype)

    @pl.when(s == 0)
    def _():
        back[:, :, 1:] = jnp.zeros(back[:, :, 1:].shape, back.dtype)

    prev[...] = jnp.zeros_like(prev)
    scales.wait()
    move.wait()
    for q in range(RB // PAIR):
        fetches[q].wait()
        densify(q, point_ref, scale_ref, blocks_ref, dense_ref, sums)
    begin.wait()
    for g in range(GROUPS):
        cur[g] = start_ref[g * PART : (g + 1) * PART, :]
    corners = 2 * (jnp.minimum(s, 1) + jnp.minimum(last - s, 1))
    down = jnp.maximum(s - 1, 0)
    up = jnp.minimum(s + 1, last)
    edge_to = [(s, before), (down, after), (down, c), (down, before)]
    back_to = [(s, after), (up, before), (up, c), (up, after)]

    def edge_copy(k, g, o):
        return pltpu.make_async_remote_copy(
            src_ref=edge.at[k, g], dst_ref=rims.at[k, g, o],
            send_sem=edge_send.at[k, g, o], recv_sem=edge_recv.at[k, g, o],
            device_id=edge_to[o], device_id_type=MESH,
        )

    def back_copy(k, g, o):
        return pltpu.make_async_remote_copy(
            src_ref=given.at[k, g, o], dst_ref=back.at[k, g, o],
            send_sem=back_send.at[k, g, o], recv_sem=back_recv.at[k, g, o],
            device_id=back_to[o], device_id_type=MESH,
        )

    def chord_copy(step):
        return pltpu.make_async_remote_copy(
            src_ref=chord_parts.at[c], dst_ref=chord_parts.at[c],
            send_sem=chord_send.at[step], recv_sem=chord_recv.at[step],
            device_id=(s, lax.rem(c + step, chords)), device_id_type=MESH,
        )

    def span_copy(step):
        return pltpu.make_async_remote_copy(
            src_ref=span_parts.at[s], dst_ref=span_parts.at[s],
            send_sem=span_send.at[step], recv_sem=span_recv.at[step],
            device_id=(lax.rem(s + step, spans), c), device_id_type=MESH,
        )

    def halo(o, inner, outer):
        if o == 0:
            inner()
        else:
            pl.when(outer)(inner)

    def rim_dense(o):
        return dense_ref[:, OWN + o * EDGE : OWN + (o + 1) * EDGE]

    def give(k, g, o, narrowed):
        given[k, g, o] = mm(narrowed, rim_dense(o)).astype(jnp.bfloat16)

    def send(k, g, ready=False):
        if not ready:
            edge[k, g] = cur[g, :, :EDGE].astype(jnp.bfloat16)
        narrowed = cur[g].astype(jnp.bfloat16)

        def issue(steps):
            for out, o in steps:
                if out:
                    halo(o, lambda o=o: edge_copy(k, g, o).start(), s > 0)
                else:
                    if not ready:
                        give(k, g, o, narrowed)
                    halo(o, lambda o=o: back_copy(k, g, o).start(), s < last)

        pl.when(c == 0)(lambda: issue(FIRST))
        pl.when(c == chords - 1)(lambda: issue(LAST))
        pl.when((c > 0) & (c < chords - 1))(lambda: issue(MIDDLE))
        if isinstance(k, int):
            for q in range(RB // HB):
                lo, hi = q * EDGE, (q + 1) * EDGE
                total[g, :, lo:hi] = mm(narrowed[:, :hi], dense_ref[:hi, lo:hi]) + mm(
                    narrowed[:, lo:], dense_ref[lo:hi, lo:OWN], NT
                )
        else:
            total[g] = mm(narrowed, mutual[...])

    def receive(k, g):

        def gather(first_part, rest):
            for part in (first_part, rest):
                for o in part:
                    halo(o, lambda o=o: edge_copy(k, g, o).wait_recv(), s < last)
                acc = total[g]
                for o in part:
                    acc = acc + mm(rims[k, g, o], across[o * EDGE : (o + 1) * EDGE, :])
                total[g] = acc

        pl.when(c == 0)(lambda: gather((2, 0, 3), (1,)))
        pl.when(c > 0)(lambda: gather((2, 1), (0, 3)))
        applied = total[g]
        for o in (2, 0, 1, 3):
            halo(o, lambda o=o: back_copy(k, g, o).wait_recv(), s > 0)
        returned = back[k, g, 0].astype(jnp.float32)
        for o in range(1, RIMS):
            returned = returned + back[k, g, o].astype(jnp.float32)
        applied = jnp.concatenate([applied[:, :EDGE] + returned, applied[:, EDGE:]], axis=1)
        first = lax.rem(k, DEG) == 0
        gain = jnp.where(first, 1.0 / SPREAD, 2.0 / SPREAD)
        keep = jnp.where(first, 0.0, 1.0)
        following = applied * gain - prev[g] * keep
        prev[g] = cur[g]
        cur[g] = following

    narrowed = cur[0].astype(jnp.bfloat16)
    edge[0, 0] = narrowed[:, :EDGE]
    for o in range(RIMS):
        give(0, 0, o, narrowed)
    pl.semaphore_wait(barrier, chords - 1 + spans - 1 + corners)
    for g in range(GROUPS):
        send(0, g, ready=g == 0)

    rows = lax.broadcasted_iota(jnp.int32, (EDGE, EDGE), 0)
    cols = lax.broadcasted_iota(jnp.int32, (EDGE, EDGE), 1)
    eye = (rows == cols).astype(jnp.bfloat16)
    for o in range(RIMS):
        across[o * EDGE : (o + 1) * EDGE, :] = mm(eye, rim_dense(o), NT).astype(jnp.bfloat16)
    for q in range(RB // HB):
        lo, hi = q * EDGE, (q + 1) * EDGE
        turned = mm(eye, dense_ref[:, lo:hi], NT)
        mutual[lo:hi, :] = (dense_ref[lo:hi, :OWN].astype(jnp.float32) + turned).astype(jnp.bfloat16)

    def drain(k):
        for g in range(GROUPS):
            for o in range(RIMS):
                halo(o, lambda o=o: edge_copy(k, g, o).wait_send(), s > 0)
                halo(o, lambda o=o: back_copy(k, g, o).wait_send(), s < last)

    def advance(k, carry):
        for g in range(GROUPS):
            receive(k - 1, g)
            send(k, g)

        @pl.when(k == DEG)
        def _():
            basis = cur[...].reshape(COLS, OWN)
            high, low = halves(basis)
            both = mm(jnp.concatenate([high, low], axis=0), high, NT)
            gram = both[:COLS] + both[COLS:] + both[COLS:].T
            chord_parts[c] = pack(gram)
            for step in range(1, chords):
                chord_copy(step).start()

        @pl.when(k == DEG + 1)
        def _():
            for step in range(1, chords):
                chord_copy(step).wait_recv()
            part = chord_parts[0]
            for step in range(1, chords):
                part = part + chord_parts[step]
            span_parts[s] = part
            for step in range(1, spans):
                span_copy(step).start()

        @pl.when(k == DEG + 2)
        def _():
            for step in range(1, spans):
                span_copy(step).wait_recv()
            part = span_parts[0]
            for step in range(1, spans):
                part = part + span_parts[step]
            part = part / float(OWN * spans * chords)
            inverse[...] = inverse_factor(unpack(part))

        drain(k - 1)
        return carry

    lax.fori_loop(1, APPS, advance, 0)
    receive(jnp.int32(APPS - 1), 0)
    drain(APPS - 1)
    for step in range(1, chords):
        chord_copy(step).wait_send()
    for step in range(1, spans):
        span_copy(step).wait_send()
    receive(jnp.int32(APPS - 1), 1)
    left, right = halves(inverse[...]), halves(cur[...].reshape(COLS, OWN))
    out_ref[...] = mm(
        jnp.concatenate([left[0], left[0], left[1]], axis=1), jnp.concatenate([right[0], right[1], right[0]], axis=0)
    )


def on_device(spans, chords, start_block, blocks, blk_col, block_scale):
    vmem = pl.BlockSpec(memory_space=pltpu.VMEM)
    dma = pltpu.SemaphoreType.DMA
    packed = (STRIP + STRIP // 4, 2 * COLS)
    split = (GROUPS, PART, OWN)
    flags = (APPS, GROUPS, RIMS)
    halos = flags + (PART, EDGE)
    return pl.pallas_call(
        functools.partial(filters, spans, chords),
        out_shape=jax.ShapeDtypeStruct((COLS, OWN), jnp.float32),
        in_specs=[pl.BlockSpec(memory_space=pl.ANY)] * 4,
        out_specs=vmem,
        scratch_shapes=[
            pltpu.VMEM((COLS, OWN), jnp.float32),
            dma,
            pltpu.VMEM(blocks.shape, jnp.bfloat16),
            dma((RB // PAIR,)),
            pltpu.SMEM(blk_col.shape, jnp.int32),
            dma,
            pltpu.SMEM(block_scale.shape, jnp.float32),
            dma,
            pltpu.VMEM((2, 8, BS), jnp.int32),
            pltpu.SMEM((2, 8, BS), jnp.int32),
            dma,
            *[pltpu.VMEM((BPR + 1, BS // 2, BS), jnp.float32)] * (2 * PAIR),
            pltpu.VMEM((OWN, WIDE), jnp.bfloat16),
            pltpu.VMEM((RIMS * EDGE, OWN), jnp.bfloat16),
            pltpu.VMEM((OWN, OWN), jnp.bfloat16),
            pltpu.VMEM(split, jnp.float32),
            pltpu.VMEM(split, jnp.float32),
            pltpu.VMEM(split, jnp.float32),
            pltpu.VMEM((APPS, GROUPS, PART, EDGE), jnp.bfloat16),
            pltpu.VMEM(halos, jnp.bfloat16),
            pltpu.VMEM(halos, jnp.bfloat16),
            pltpu.VMEM(halos, jnp.bfloat16),
            pltpu.VMEM((COLS, COLS), jnp.float32),
            pltpu.VMEM((chords,) + packed, jnp.float32),
            pltpu.VMEM((spans,) + packed, jnp.float32),
            dma(flags), dma(flags), dma(flags), dma(flags),
            dma((chords,)), dma((chords,)), dma((spans,)), dma((spans,)),
        ],
        compiler_params=pltpu.CompilerParams(
            collective_id=0, has_side_effects=True, vmem_limit_bytes=48 * 1024 * 1024
        ),
        name="filters",
    )(
        *[pltpu.with_memory_space_constraint(array, pltpu.HBM) for array in (start_block, blocks, blk_col, block_scale)]
    )


def solution(mesh):
    in_specs = (
        P(None, ("span", "chord")),
        P(("span", "chord"), None, None),
        P(("span", "chord")),
        P(("span", "chord")),
    )
    out_specs = P(None, ("span", "chord"))
    return jax.shard_map(
        functools.partial(on_device, mesh.shape["span"], mesh.shape["chord"]),
        mesh=mesh, in_specs=in_specs, out_specs=out_specs, check_vma=False,
    )
```
